32 devices in a mesh: grp: 8 (over z, x), tp: 4 (over y, core).
Axes of the slice: x: 2, y: 2, z: 4, core: 2. Of those that a mesh axis runs over, the one named last changes fastest.
Arguments:
- suffix_cache: bfloat16 [32, 512, 2, 1024], P('grp', None, None, 'tp'), may hold values from -6 to 6
- prompt_cache: bfloat16 [16, 512, 2, 1024], P('grp', None, None, 'tp'), may hold values from -6 to 6
- query_first: bfloat16 [32, 8192], P('grp', 'tp'), may hold values from -45 to 45
- fresh_first: bfloat16 [32, 2, 1024], P('grp', None, 'tp'), may hold values from -6 to 6
- query_second: bfloat16 [32, 8192], P('grp', 'tp'), may hold values from -45 to 45
- fresh_second: bfloat16 [32, 2, 1024], P('grp', None, 'tp'), may hold values from -6 to 6
- out_weight: bfloat16 [8192, 4096], P('tp'), may hold values from -1 to 1
- suffix_len: int32 [32], replicated, may hold values from 0 to 511, as said below
- prompt_slot: int32 [32], P('grp'), may hold values from -1 to 1, as said below
- moves: int32 [2, 5], replicated, may hold values from 0 to 7, as said below
Outputs:
- out_first: bfloat16 [32, 4096], P('grp', 'tp')
- out_second: bfloat16 [32, 4096], P('grp', 'tp')
The draws below stay inside these ranges and needn't reach their ends.
Inputs may be any that keep to these rules, and one draw needn't show every extreme that they name: `suffix_len`: 0 exactly on empty slots, 1 or more on live ones. Every group has exactly one empty slot before the migration. The source of every move is live and its length is 384 or more; some source has 511. `prompt_slot`: each group's live samples read its prompt slots; in every destination group all live samples read one prompt slot and the other is free. `moves`: source groups are distinct, destination groups are distinct, and no group is both. The destination slot is the destination group's empty slot and the destination prompt slot is its free prompt slot.
All inputs are finite; a program needn't handle non-finite values.
Results may differ from the reference program's by a relative error of at most 0.0058.
Values may be sent and summed in bfloat16 or wider, within the bound.
A program may use at most 128 MiB of HBM per device.

```python
import jax
import jax.numpy as jnp
from jax import lax

QH = 64
KVH = 8
HD = 128
DOUT = 4096
SLOTS = 4
SUF = 512
PROMPT = 512
PSLOTS = 2
N_GRP_SAMPLES = 32
MOVES = 2
N_GRP = 8


def layout_tables(key):
    streams = jax.random.split(jax.random.fold_in(key, 7), 9)
    half = N_GRP // 2
    residues = jax.random.permutation(streams[0], half)[:MOVES]
    upper = jax.random.randint(streams[7], (MOVES,), 0, 2)
    sources = residues + upper * half
    partners = residues + (1 - upper) * half
    odd_count = MOVES // 2
    odd_order = jax.random.permutation(streams[8], odd_count)
    mapping = jnp.arange(MOVES).at[2 * jnp.arange(odd_count) + 1].set(2 * odd_order + 1)
    targets = partners[mapping]
    empty_slot = jax.random.randint(streams[1], (N_GRP,), 0, SLOTS)
    source_slot = (empty_slot[sources] + 1 + jax.random.randint(streams[2], (MOVES,), 0, SLOTS - 1)) % SLOTS
    target_slot = empty_slot[targets]
    free_prompt = jax.random.randint(streams[3], (N_GRP,), 0, 2)
    target_prompt = free_prompt[targets]
    is_target = jnp.zeros((N_GRP,), jnp.int32).at[targets].set(1)
    usage = jax.random.randint(streams[4], (N_GRP, SLOTS), 0, 2)
    usage = jnp.where(is_target[:, None] == 1, 1 - free_prompt[:, None], usage)
    slot_ids = jnp.arange(SLOTS)[None, :]
    prompt_ids = jnp.where(slot_ids == empty_slot[:, None], -1, usage)
    lengths = jax.random.randint(streams[5], (N_GRP, SLOTS), 1, SUF)
    long_lengths = jax.random.randint(streams[6], (MOVES,), 3 * SUF // 4, SUF)
    long_lengths = long_lengths.at[0].set(SUF - 1)
    lengths = lengths.at[sources, source_slot].set(long_lengths)
    lengths = jnp.where(slot_ids == empty_slot[:, None], 0, lengths)
    move_rows = jnp.stack([sources, source_slot, targets, target_slot, target_prompt], 1).astype(jnp.int32)
    return (lengths.reshape(-1).astype(jnp.int32), prompt_ids.reshape(-1).astype(jnp.int32), move_rows)


def float_draws(key):
    streams = jax.random.split(jax.random.fold_in(key, 23), 3)
    prompt_shape = (N_GRP * PSLOTS, PROMPT, 2, KVH * HD)
    query_shape = (N_GRP * SLOTS, QH * HD)
    prompt = jnp.clip(jax.random.normal(streams[0], prompt_shape, jnp.float32), -6.0, 6.0)
    first = jnp.clip(jax.random.normal(streams[1], query_shape, jnp.float32), -6.0, 6.0)
    second = jnp.clip(jax.random.normal(streams[2], query_shape, jnp.float32), -6.0, 6.0)
    return (prompt, first, second)


def draw_prompt_cache(key, part):
    return float_draws(key)[0].astype(jnp.bfloat16)


def draw_query_first(key, part):
    return float_draws(key)[1].astype(jnp.bfloat16)


def draw_query_second(key, part):
    return float_draws(key)[2].astype(jnp.bfloat16)


def draw_suffix_len(key, part):
    return layout_tables(key)[0]


def draw_prompt_slot(key, part):
    return layout_tables(key)[1]


def draw_moves(key, part):
    return layout_tables(key)[2]


def levels(own_key, dims, cuts, least, largest):
    gain, own = 1.0, jax.random.fold_in(own_key, 6)
    for position, parts in cuts:
        draws = jnp.exp(jax.random.uniform(jax.random.fold_in(own, position), (parts,), jnp.float32, least / len(cuts), largest / len(cuts)))
        gain = gain * jnp.repeat(draws, dims[position] // parts).reshape([-1 if axis == position else 1 for axis in range(len(dims))])
    return gain


def bell_draw(key, extent, deviation, most, cuts=(), held_as=jnp.bfloat16):
    loudness = levels(key, extent, cuts, -0.22, 0.18) if cuts else 1.0
    array = jax.random.normal(key, extent, jnp.float32) * deviation * loudness
    return jnp.minimum(jnp.maximum(array, -most), most).astype(held_as)


def setup_inputs(seed: int = 0) -> dict:
    arg_keys = jax.random.split(jax.random.key(seed), 11)
    return {
        "suffix_cache": bell_draw(arg_keys[0], (N_GRP_SAMPLES, SUF, 2, KVH * HD), 1.0, 6.0, ((0, 8), (3, 4))),
        "prompt_cache": draw_prompt_cache(jax.random.fold_in(arg_keys[10], 71), 0),
        "query_first": draw_query_first(jax.random.fold_in(arg_keys[10], 71), 0),
        "fresh_first": bell_draw(arg_keys[3], (N_GRP_SAMPLES, 2, KVH * HD), 1.0, 6.0, ((0, 8), (2, 4))),
        "query_second": draw_query_second(jax.random.fold_in(arg_keys[10], 71), 0),
        "fresh_second": bell_draw(arg_keys[5], (N_GRP_SAMPLES, 2, KVH * HD), 1.0, 6.0, ((0, 8), (2, 4))),
        "out_weight": bell_draw(arg_keys[6], (QH * HD, DOUT), (HD // 4) ** -0.5, 1.0, ((0, 4),)),
        "suffix_len": draw_suffix_len(jax.random.fold_in(arg_keys[10], 71), 0),
        "prompt_slot": draw_prompt_slot(jax.random.fold_in(arg_keys[10], 71), 0),
        "moves": draw_moves(jax.random.fold_in(arg_keys[10], 71), 0),
    }


def attend_sample(queries, prompt_kv, suffix_kv, fresh, length):
    key_rows = jnp.concatenate([prompt_kv[:, 0], suffix_kv[:, 0], fresh[None, 0]], 0).astype(jnp.float32)
    value_rows = jnp.concatenate([prompt_kv[:, 1], suffix_kv[:, 1], fresh[None, 1]], 0).astype(jnp.float32)
    total_rows = key_rows.shape[0]
    key_rows = key_rows.reshape(total_rows, KVH, HD)
    value_rows = value_rows.reshape(total_rows, KVH, HD)
    heads = queries.astype(jnp.float32).reshape(KVH, QH // KVH, HD)
    scores = jnp.einsum("kgd,lkd->kgl", heads, key_rows) * (HD ** -0.5)
    valid = jnp.concatenate([jnp.ones((PROMPT,), bool), jnp.arange(SUF, dtype=jnp.int32) < length, jnp.ones((1,), bool)])
    scores = jnp.where(valid[None, None, :], scores, -1e30)
    highest = jnp.max(scores, -1, keepdims=True)
    spread = jnp.exp(scores - highest)
    weights = (spread / jnp.sum(spread, -1, keepdims=True)).astype(jnp.bfloat16)
    weights = lax.optimization_barrier(weights).astype(jnp.float32)
    mixed = jnp.einsum("kgl,lkd->kgd", weights, value_rows)
    return mixed.reshape(QH * HD)


def decode_all(queries, prompt_cache, suffix_cache, fresh, lengths, prompt_ids):
    def one_sample(sample):
        prompt_row = (sample // SLOTS) * PSLOTS + jnp.maximum(prompt_ids[sample], 0)
        result = attend_sample(queries[sample], prompt_cache[prompt_row], suffix_cache[sample], fresh[sample], lengths[sample])
        return jnp.where(prompt_ids[sample] >= 0, result, 0.0).astype(jnp.bfloat16)

    return lax.map(one_sample, jnp.arange(queries.shape[0], dtype=jnp.int32))


def reference(suffix_cache, prompt_cache, query_first, fresh_first, query_second, fresh_second, out_weight, suffix_len, prompt_slot, moves):
    attn_first = decode_all(query_first, prompt_cache, suffix_cache, fresh_first, suffix_len, prompt_slot)
    positions = jnp.arange(SUF, dtype=jnp.int32)
    write_mask = (positions[None, :] == suffix_len[:, None]) & (prompt_slot[:, None] >= 0)
    appended = jnp.where(write_mask[:, :, None, None], fresh_first[:, None], suffix_cache)
    source_rows = (moves[:, 0] * SLOTS + moves[:, 1]).astype(jnp.int32)
    target_rows = (moves[:, 2] * SLOTS + moves[:, 3]).astype(jnp.int32)
    prompt_from = (moves[:, 0] * PSLOTS + prompt_slot[source_rows]).astype(jnp.int32)
    prompt_into = (moves[:, 2] * PSLOTS + moves[:, 4]).astype(jnp.int32)
    suffix_moved = appended.at[target_rows].set(appended[source_rows])
    prompt_moved = prompt_cache.at[prompt_into].set(prompt_cache[prompt_from])
    grown = jnp.where(prompt_slot >= 0, suffix_len + 1, 0).astype(jnp.int32)
    length_moved = grown.at[target_rows].set(grown[source_rows]).at[source_rows].set(0)
    slot_moved = prompt_slot.at[target_rows].set(moves[:, 4]).at[source_rows].set(-1)
    attn_second = decode_all(query_second, prompt_moved, suffix_moved, fresh_second, length_moved, slot_moved)
    out_first = jnp.dot(attn_first, out_weight, preferred_element_type=jnp.float32).astype(jnp.bfloat16)
    out_second = jnp.dot(attn_second, out_weight, preferred_element_type=jnp.float32).astype(jnp.bfloat16)
    return out_first, out_second
```

```python
import functools

import jax
import jax.numpy as jnp
from jax import lax
from jax.experimental import pallas as pl
from jax.experimental.pallas import tpu as pltpu
from jax.sharding import PartitionSpec as P

QH = 64
KVH = 8
HD = 128
MESH = pl.DeviceIdType.MESH
F32 = jnp.float32
BF16 = jnp.bfloat16


def kernel(
    groups,
    ranks,
    lens_ref,
    pslot_ref,
    moves_ref,
    suffix_hbm,
    prompt_hbm,
    q1_ref,
    f1_ref,
    q2_ref,
    f2_ref,
    weight_hbm,
    out_ref,
    sbuf,
    pbuf,
    wbuf,
    qs,
    fs,
    packets,
    parts_out,
    parts_in,
    rows_back,
    kv_sem,
    w_sem,
    g_send,
    g_recv,
    r_send,
    r_recv,
    b_send,
    b_recv,
):
    me = lax.axis_index("grp")
    rank = lax.axis_index("tp")
    slots = q1_ref.shape[0]
    prompts = prompt_hbm.shape[0]
    features = q1_ref.shape[1]
    heads = features // HD
    share = QH // KVH
    kv_heads = heads // share
    width = kv_heads * HD
    cap = suffix_hbm.shape[1]
    plen = prompt_hbm.shape[1]
    cols = out_ref.shape[1]
    move_count = moves_ref.shape[0]

    def kv_copies():
        copies = []
        for k in range(kv_heads):
            lanes = pl.ds(k * HD, HD)
            for p in range(prompts):
                copies.append(
                    pltpu.make_async_copy(
                        prompt_hbm.at[p, :, :, lanes], pbuf.at[p, k], kv_sem.at[p, k]
                    )
                )
            for s in range(slots):
                copies.append(
                    pltpu.make_async_copy(
                        suffix_hbm.at[s, :, :, lanes], sbuf.at[s, k], kv_sem.at[prompts + s, k]
                    )
                )
        return copies

    def weight_copy(t):
        j = lax.rem(rank + t, ranks)
        return pltpu.make_async_copy(
            weight_hbm.at[:, pl.ds(pl.multiple_of(j * cols, cols), cols)], wbuf.at[t], w_sem.at[t]
        )

    barrier = pltpu.get_barrier_semaphore()
    for t in range(1, groups):
        pl.semaphore_signal(
            barrier, inc=1, device_id=(lax.rem(me + t, groups), rank), device_id_type=MESH
        )
    for t in range(1, ranks):
        pl.semaphore_signal(
            barrier, inc=1, device_id=(me, lax.rem(rank + t, ranks)), device_id_type=MESH
        )

    for copy in kv_copies():
        copy.start()
    steps = [t % ranks for t in range(1, ranks + 1)]
    for t in steps:
        weight_copy(t).start()

    zero = jnp.int32(0)
    out_slot, into_group, in_slot, from_group = zero - 1, zero, zero - 1, zero
    for m in range(move_count):
        leaves = moves_ref[m, 0] == me
        enters = moves_ref[m, 2] == me
        out_slot = jnp.where(leaves, moves_ref[m, 1], out_slot)
        into_group = jnp.where(leaves, moves_ref[m, 2], into_group)
        in_slot = jnp.where(enters, moves_ref[m, 3], in_slot)
        from_group = jnp.where(enters, moves_ref[m, 0], from_group)

    q2 = q2_ref[...].astype(F32)
    row_ids = lax.broadcasted_iota(jnp.int32, (slots, 1), 0)
    own_row = jnp.sum(jnp.where(row_ids == in_slot, q2, 0.0), 0, keepdims=True)
    fresh2 = [f2_ref[s].astype(F32) for s in range(slots)]
    own_fresh = jnp.zeros((2, width), F32)
    for s in range(slots):
        own_fresh = jnp.where(in_slot == s, fresh2[s], own_fresh)
    packets[me, :, :features] = own_row
    packets[me, :, features : features + width] = own_fresh[0:1]
    packets[me, :, features + width :] = own_fresh[1:2]

    pl.semaphore_wait(barrier, groups - 1 + ranks - 1)

    def gather_copy(t):
        return pltpu.make_async_remote_copy(
            src_ref=packets.at[me],
            dst_ref=packets.at[me],
            send_sem=g_send.at[t],
            recv_sem=g_recv.at[t],
            device_id=(lax.rem(me + t, groups), rank),
            device_id_type=MESH,
        )

    for t in range(1, groups):
        gather_copy(t).start()

    qs[0:slots] = q1_ref[...].astype(F32)
    for s in range(slots):
        fs[s, 0:2] = f1_ref[s].astype(F32)

    for t in range(1, groups):
        gather_copy(t).wait()

    foreign = packets[into_group]
    qs[slots : 2 * slots] = jnp.where(row_ids == out_slot, foreign[:, :features], q2)
    foreign_fresh = jnp.concatenate(
        [foreign[:, features : features + width], foreign[:, features + width :]], 0
    )
    for s in range(slots):
        fs[s, 2:4] = jnp.where(out_slot == s, foreign_fresh, fresh2[s])
        fs[s, 4:8] = jnp.zeros((4, width), F32)

    rows = 2 * slots
    total = heads * rows
    mine = 2 * heads
    stacked = jnp.concatenate([qs[:, j * HD : (j + 1) * HD] for j in range(heads)], 0).astype(BF16)
    def source_of(r):
        s = r // mine
        k = (r % mine) // (2 * share)
        step = (r % (2 * share)) // share
        g = r % share
        return (k * share + g) * rows + step * slots + s

    swap = (
        source_of(lax.broadcasted_iota(jnp.int32, (total, total), 0))
        == lax.broadcasted_iota(jnp.int32, (total, total), 1)
    ).astype(F32).astype(BF16)
    back = (
        source_of(lax.broadcasted_iota(jnp.int32, (total, total), 1))
        == lax.broadcasted_iota(jnp.int32, (total, total), 0)
    ).astype(F32).astype(BF16)
    queries = jnp.dot(swap, stacked, preferred_element_type=F32)

    for copy in kv_copies():
        copy.wait()

    scale = HD ** (-0.5)
    nt = (((1,), (1,)), ((), ()))
    q_row = lax.broadcasted_iota(jnp.int32, (mine, 1), 0)
    second = (q_row % (2 * share)) >= share
    p_col = lax.broadcasted_iota(jnp.int32, (1, 2 * plen), 1)
    s_col = lax.broadcasted_iota(jnp.int32, (1, 2 * cap), 1)
    f_col = lax.broadcasted_iota(jnp.int32, (1, 8), 1)
    p_valid = (p_col % 2) == 0
    f_valid = (f_col == 0) | ((f_col == 2) & second)
    low = -1e30
    results = []
    for s in range(slots):
        q = queries[s * mine : (s + 1) * mine]
        wide = jnp.concatenate(
            [
                jnp.where((q_row // (2 * share)) == k, q, 0.0)
                for k in range(kv_heads)
            ],
            1,
        ).astype(BF16)
        chosen = pslot_ref[s]
        live = chosen >= 0
        row = jnp.maximum(chosen, 0)
        n = lens_ref[me * slots + s]
        xp = jnp.concatenate(
            [pbuf.reshape(prompts, kv_heads, 2 * plen, HD)[row, k] for k in range(kv_heads)], 1
        )
        xs = jnp.concatenate(
            [sbuf.reshape(slots, kv_heads, 2 * cap, HD)[s, k] for k in range(kv_heads)], 1
        )
        xf = fs[s].astype(BF16)
        sp = lax.dot_general(wide, xp, nt, preferred_element_type=F32) * scale
        ss = lax.dot_general(wide, xs, nt, preferred_element_type=F32) * scale
        sf = lax.dot_general(wide, xf, nt, preferred_element_type=F32) * scale
        s_valid = ((s_col % 2) == 0) & (s_col < 2 * n)
        sp = jnp.where(p_valid, sp, low)
        ss = jnp.where(s_valid, ss, low)
        sf = jnp.where(f_valid, sf, low)
        top = jnp.maximum(
            jnp.maximum(jnp.max(sp, 1, keepdims=True), jnp.max(ss, 1, keepdims=True)),
            jnp.max(sf, 1, keepdims=True),
        )
        ep, es, ef = jnp.exp(sp - top), jnp.exp(ss - top), jnp.exp(sf - top)
        sum_all = (
            jnp.sum(ep, 1, keepdims=True)
            + jnp.sum(es, 1, keepdims=True)
            + jnp.sum(ef, 1, keepdims=True)
        )
        inv = 1.0 / sum_all

        def shifted(e):
            w = e * inv
            return jnp.concatenate(
                [
                    pltpu.roll(w[:, i : i + HD], 1, 1)
                    for i in range(0, e.shape[1], HD)
                ],
                1,
            ).astype(BF16)

        mixed = jnp.dot(shifted(ep), xp, preferred_element_type=F32)
        mixed += jnp.dot(shifted(es), xs, preferred_element_type=F32)
        wf = (ef * inv).astype(BF16).astype(F32)
        fval = fs[s]
        mixed += wf[:, 0:1] * fval[1:2] + wf[:, 2:3] * fval[3:4]
        picked = mixed[:, :HD]
        for k in range(1, kv_heads):
            picked = jnp.where((q_row // (2 * share)) == k, mixed[:, k * HD : (k + 1) * HD], picked)
        results.append(jnp.where(live, picked, 0.0))
    attn = jnp.concatenate(results, 0).astype(BF16)
    attn = jnp.dot(back, attn, preferred_element_type=F32)
    attn = jnp.concatenate([attn[j * rows : (j + 1) * rows] for j in range(heads)], 1).astype(BF16)

    def part_copy(t):
        return pltpu.make_async_remote_copy(
            src_ref=parts_out.at[t],
            dst_ref=parts_in.at[t],
            send_sem=r_send.at[t],
            recv_sem=r_recv.at[t],
            device_id=(me, lax.rem(rank + t, ranks)),
            device_id_type=MESH,
        )

    result = None
    for t in steps:
        weight_copy(t).wait()
        part = jnp.dot(attn, wbuf[t], preferred_element_type=F32)
        if t:
            parts_out[t] = part.astype(BF16)
            part_copy(t).start()
        else:
            result = part
    for t in range(1, ranks):
        part_copy(t).wait()
        result += parts_in[t].astype(F32)

    out_rows = lax.broadcasted_iota(jnp.int32, (rows, 1), 0)
    going = (out_rows == slots + out_slot) & (out_slot >= 0)
    rows_back[me] = jnp.sum(jnp.where(going, result, 0.0), 0, keepdims=True)

    def back_copy(t):
        return pltpu.make_async_remote_copy(
            src_ref=rows_back.at[me],
            dst_ref=rows_back.at[me],
            send_sem=b_send.at[t],
            recv_sem=b_recv.at[t],
            device_id=(lax.rem(me + t, groups), rank),
            device_id_type=MESH,
        )

    for t in range(1, groups):
        back_copy(t).start()
    for t in range(1, groups):
        back_copy(t).wait()
    coming = (out_rows == slots + in_slot) & (in_slot >= 0)
    result = jnp.where(coming, rows_back[from_group], jnp.where(going, 0.0, result))
    out_ref[...] = result.astype(BF16)


def per_device(
    suffix_cache,
    prompt_cache,
    query_first,
    fresh_first,
    query_second,
    fresh_second,
    out_weight,
    suffix_len,
    prompt_slot,
    moves,
):
    groups, ranks = lax.axis_size("grp"), lax.axis_size("tp")
    slots, features = query_first.shape
    prompts, plen = prompt_cache.shape[:2]
    cap = suffix_cache.shape[1]
    width = suffix_cache.shape[3]
    kv_heads = width // HD
    cols = out_weight.shape[1] // ranks
    depth = out_weight.shape[0]
    vmem = pl.BlockSpec(memory_space=pltpu.VMEM)
    smem = pl.BlockSpec(memory_space=pltpu.SMEM)
    hbm = pl.BlockSpec(memory_space=pltpu.HBM)
    dma = pltpu.SemaphoreType.DMA
    out = pl.pallas_call(
        functools.partial(kernel, groups, ranks),
        out_shape=jax.ShapeDtypeStruct((2 * slots, cols), BF16),
        in_specs=[smem, smem, smem, hbm, hbm, vmem, vmem, vmem, vmem, hbm],
        out_specs=vmem,
        scratch_shapes=[
            pltpu.VMEM((slots, kv_heads, cap, 2, HD), BF16),
            pltpu.VMEM((prompts, kv_heads, plen, 2, HD), BF16),
            pltpu.VMEM((ranks, depth, cols), BF16),
            pltpu.VMEM((2 * slots, features), F32),
            pltpu.VMEM((slots, 8, width), F32),
            pltpu.VMEM((groups, 1, features + 2 * width), F32),
            pltpu.VMEM((ranks, 2 * slots, cols), BF16),
            pltpu.VMEM((ranks, 2 * slots, cols), BF16),
            pltpu.VMEM((groups, 1, cols), F32),
            dma((prompts + slots, kv_heads)),
            dma((ranks,)),
            dma((groups,)),
            dma((groups,)),
            dma((ranks,)),
            dma((ranks,)),
            dma((groups,)),
            dma((groups,)),
        ],
        compiler_params=pltpu.CompilerParams(
            collective_id=0, has_side_effects=True, vmem_limit_bytes=48 * 1024 * 1024
        ),
    )(
        suffix_len,
        prompt_slot,
        moves,
        suffix_cache,
        prompt_cache,
        query_first,
        fresh_first,
        query_second,
        fresh_second,
        out_weight,
    )
    return out[:slots], out[slots:]


def solution(mesh):
    placed = (
        P("grp", None, None, "tp"),
        P("grp", None, None, "tp"),
        P("grp", "tp"),
        P("grp", None, "tp"),
        P("grp", "tp"),
        P("grp", None, "tp"),
        P("tp", None),
        P(),
        P("grp"),
        P(),
    )
    return jax.shard_map(
        per_device,
        mesh=mesh,
        in_specs=placed,
        out_specs=(P("grp", "tp"), P("grp", "tp")),
        check_vma=False,
    )
```

```python
import functools

import jax
import jax.numpy as jnp
from jax import lax
from jax.experimental import pallas as pl
from jax.experimental.pallas import tpu as pltpu
from jax.sharding import PartitionSpec as P

QH = 64
KVH = 8
HD = 128
MESH = pl.DeviceIdType.MESH
F32 = jnp.float32
BF16 = jnp.bfloat16


def kernel(
    groups,
    ranks,
    suffix_hbm,
    prompt_hbm,
    q1_hbm,
    f1_hbm,
    q2_hbm,
    f2_hbm,
    weight_hbm,
    lens_hbm,
    pslot_hbm,
    moves_hbm,
    out_ref,
    sbuf,
    pbuf,
    wbuf,
    q1_ref,
    f1_ref,
    q2_ref,
    f2_ref,
    lens_ref,
    pslot_ref,
    moves_ref,
    qs,
    fs,
    fresh_in,
    packets,
    parts_out,
    parts_in,
    rows_back,
    small_sem,
    kv_sem,
    w_sem,
    g_send,
    g_recv,
    r_send,
    r_recv,
    b_send,
    b_recv,
):
    me = lax.axis_index("grp")
    rank = lax.axis_index("tp")
    slots = q1_ref.shape[0]
    prompts = prompt_hbm.shape[0]
    features = q1_ref.shape[1]
    heads = features // HD
    share = QH // KVH
    kv_heads = heads // share
    width = kv_heads * HD
    cap = suffix_hbm.shape[1]
    plen = prompt_hbm.shape[1]
    cols = out_ref.shape[1]
    move_count = moves_ref.shape[0]

    barrier = pltpu.get_barrier_semaphore()
    for t in range(1, groups):
        pl.semaphore_signal(
            barrier, inc=1, device_id=(lax.rem(me + t, groups), rank), device_id_type=MESH
        )
    for t in range(1, ranks):
        pl.semaphore_signal(
            barrier, inc=1, device_id=(me, lax.rem(rank + t, ranks)), device_id_type=MESH
        )

    small = [
        pltpu.make_async_copy(src, dst, small_sem.at[i])
        for i, (src, dst) in enumerate(
            [
                (moves_hbm, moves_ref),
                (q2_hbm, q2_ref),
                (f2_hbm, f2_ref),
                (lens_hbm, lens_ref),
                (pslot_hbm, pslot_ref),
                (q1_hbm, q1_ref),
                (f1_hbm, f1_ref),
            ]
        )
    ]
    kv_copies = []
    for k in range(kv_heads):
        lanes = pl.ds(k * HD, HD)
        for p in range(prompts):
            kv_copies.append(
                pltpu.make_async_copy(
                    prompt_hbm.at[p, :, :, lanes], pbuf.at[p, k], kv_sem.at[p, k]
                )
            )
        for s in range(slots):
            kv_copies.append(
                pltpu.make_async_copy(
                    suffix_hbm.at[s, :, :, lanes], sbuf.at[s, k], kv_sem.at[prompts + s, k]
                )
            )

    def weight_copy(t):
        j = lax.rem(rank + t, ranks)
        return pltpu.make_async_copy(
            weight_hbm.at[:, pl.ds(pl.multiple_of(j * cols, cols), cols)], wbuf.at[t], w_sem.at[t]
        )

    steps = [t % ranks for t in range(1, ranks + 1)]
    for copy in small:
        copy.start()
    for copy in kv_copies:
        copy.start()
    for t in steps:
        weight_copy(t).start()
    for copy in small:
        copy.wait()

    zero = jnp.int32(0)
    out_slot, into_group, in_slot, from_group = zero - 1, zero, zero - 1, zero
    for m in range(move_count):
        leaves = moves_ref[m, 0] == me
        enters = moves_ref[m, 2] == me
        out_slot = jnp.where(leaves, moves_ref[m, 1], out_slot)
        into_group = jnp.where(leaves, moves_ref[m, 2], into_group)
        in_slot = jnp.where(enters, moves_ref[m, 3], in_slot)
        from_group = jnp.where(enters, moves_ref[m, 0], from_group)

    rows = 2 * slots
    qs[0:slots] = q1_ref[...].astype(F32)
    qs[slots:rows] = q2_ref[...].astype(F32)
    stacked = jnp.concatenate([qs[:, j * HD : (j + 1) * HD] for j in range(heads)], 0).astype(BF16)
    total = heads * rows

    pick = (
        lax.broadcasted_iota(jnp.int32, (heads, total), 1)
        == lax.broadcasted_iota(jnp.int32, (heads, total), 0) * rows + slots + in_slot
    ).astype(F32).astype(BF16)
    packets[me, 0:heads] = jnp.dot(pick, stacked, preferred_element_type=F32)
    fresh2 = [f2_ref[s].astype(F32) for s in range(slots)]
    own_fresh = jnp.zeros((2, width), F32)
    for s in range(slots):
        own_fresh = jnp.where(in_slot == s, fresh2[s], own_fresh)
    for k in range(kv_heads):
        packets[me, heads + 2 * k : heads + 2 * k + 2] = own_fresh[:, k * HD : (k + 1) * HD]

    pl.semaphore_wait(barrier, groups - 1 + ranks - 1)

    def gather_copy(t):
        return pltpu.make_async_remote_copy(
            src_ref=packets.at[me],
            dst_ref=packets.at[me],
            send_sem=g_send.at[t],
            recv_sem=g_recv.at[t],
            device_id=(lax.rem(me + t, groups), rank),
            device_id_type=MESH,
        )

    for t in range(1, groups):
        gather_copy(t).start()

    for s in range(slots):
        fs[s, 0:2] = f1_ref[s].astype(F32)
        fs[s, 2:4] = fresh2[s]
        fs[s, 4:8] = jnp.zeros((4, width), F32)

    mine = 2 * heads

    def source_of(r):
        s = r // mine
        k = (r % mine) // (2 * share)
        step = (r % (2 * share)) // share
        g = r % share
        return (k * share + g) * rows + step * slots + s

    swap = (
        source_of(lax.broadcasted_iota(jnp.int32, (total, total), 0))
        == lax.broadcasted_iota(jnp.int32, (total, total), 1)
    ).astype(F32).astype(BF16)
    back = (
        source_of(lax.broadcasted_iota(jnp.int32, (total, total), 1))
        == lax.broadcasted_iota(jnp.int32, (total, total), 0)
    ).astype(F32).astype(BF16)
    queries = jnp.dot(swap, stacked, preferred_element_type=F32)

    for copy in kv_copies:
        copy.wait()

    scale = HD ** (-0.5)
    low = -1e30
    nt = (((1,), (1,)), ((), ()))
    flat_p = pbuf.reshape(prompts, kv_heads, 2 * plen, HD)
    flat_s = sbuf.reshape(slots, kv_heads, 2 * cap, HD)
    p_col = lax.broadcasted_iota(jnp.int32, (1, 2 * plen), 1)
    s_col = lax.broadcasted_iota(jnp.int32, (1, 2 * cap), 1)
    f_col = lax.broadcasted_iota(jnp.int32, (1, 8), 1)
    p_valid = (p_col % 2) == 0
    s_even = (s_col % 2) == 0

    def attend(q, head_of, second, s, fval):
        wide = jnp.concatenate(
            [jnp.where(head_of == k, q, 0.0) for k in range(kv_heads)], 1
        ).astype(BF16)
        row = jnp.maximum(pslot_ref[s], 0)
        n = lens_ref[me * slots + s]
        xp = jnp.concatenate([flat_p[row, k] for k in range(kv_heads)], 1)
        xs = jnp.concatenate([flat_s[s, k] for k in range(kv_heads)], 1)
        xf = fval.astype(BF16)
        sp = lax.dot_general(wide, xp, nt, preferred_element_type=F32) * scale
        ss = lax.dot_general(wide, xs, nt, preferred_element_type=F32) * scale
        sf = lax.dot_general(wide, xf, nt, preferred_element_type=F32) * scale
        sp = jnp.where(p_valid, sp, low)
        ss = jnp.where(s_even & (s_col < 2 * n), ss, low)
        sf = jnp.where((f_col == 0) | ((f_col == 2) & second), sf, low)
        top = jnp.maximum(
            jnp.maximum(jnp.max(sp, 1, keepdims=True), jnp.max(ss, 1, keepdims=True)),
            jnp.max(sf, 1, keepdims=True),
        )
        ep, es, ef = jnp.exp(sp - top), jnp.exp(ss - top), jnp.exp(sf - top)
        inv = 1.0 / (
            jnp.sum(ep, 1, keepdims=True)
            + jnp.sum(es, 1, keepdims=True)
            + jnp.sum(ef, 1, keepdims=True)
        )

        def shifted(e):
            w = e * inv
            return jnp.concatenate(
                [pltpu.roll(w[:, i : i + HD], 1, 1) for i in range(0, e.shape[1], HD)], 1
            ).astype(BF16)

        mixed = jnp.dot(shifted(ep), xp, preferred_element_type=F32)
        mixed += jnp.dot(shifted(es), xs, preferred_element_type=F32)
        wf = (ef * inv).astype(BF16).astype(F32)
        mixed += wf[:, 0:1] * fval[1:2] + wf[:, 2:3] * fval[3:4]
        picked = mixed[:, :HD]
        for k in range(1, kv_heads):
            picked = jnp.where(head_of == k, mixed[:, k * HD : (k + 1) * HD], picked)
        return jnp.where(pslot_ref[s] >= 0, picked, 0.0)

    q_row = lax.broadcasted_iota(jnp.int32, (mine, 1), 0)
    results = [
        attend(
            queries[s * mine : (s + 1) * mine],
            q_row // (2 * share),
            (q_row % (2 * share)) >= share,
            s,
            fs[s],
        )
        for s in range(slots)
    ]
    attn = jnp.concatenate(results, 0).astype(BF16)
    attn = jnp.dot(back, attn, preferred_element_type=F32)

    for t in range(1, groups):
        gather_copy(t).wait()
    leaver = jnp.maximum(out_slot, 0)
    foreign = packets[into_group]
    fresh_in[...] = jnp.zeros((8, width), F32)
    for k in range(kv_heads):
        fresh_in[2:4, k * HD : (k + 1) * HD] = foreign[heads + 2 * k : heads + 2 * k + 2]
    fresh_in[0:2] = f1_ref[leaver].astype(F32)
    h_row = lax.broadcasted_iota(jnp.int32, (heads, 1), 0)
    guest = attend(foreign[:heads], h_row // share, h_row >= 0, leaver, fresh_in[...])
    r_row = lax.broadcasted_iota(jnp.int32, (rows, 1), 0)
    going = (r_row == slots + out_slot) & (out_slot >= 0)
    attn = jnp.concatenate(
        [
            jnp.where(going, guest[j : j + 1], attn[j * rows : (j + 1) * rows])
            for j in range(heads)
        ],
        1,
    ).astype(BF16)

    def part_copy(t):
        return pltpu.make_async_remote_copy(
            src_ref=parts_out.at[t],
            dst_ref=parts_in.at[t],
            send_sem=r_send.at[t],
            recv_sem=r_recv.at[t],
            device_id=(me, lax.rem(rank + t, ranks)),
            device_id_type=MESH,
        )

    result = None
    for t in steps:
        weight_copy(t).wait()
        part = jnp.dot(attn, wbuf[t], preferred_element_type=F32)
        if t:
            parts_out[t] = part.astype(BF16)
            part_copy(t).start()
        else:
            result = part
    for t in range(1, ranks):
        part_copy(t).wait()
        result += parts_in[t].astype(F32)

    rows_back[me] = jnp.sum(jnp.where(going, result, 0.0), 0, keepdims=True)

    def back_copy(t):
        return pltpu.make_async_remote_copy(
            src_ref=rows_back.at[me],
            dst_ref=rows_back.at[me],
            send_sem=b_send.at[t],
            recv_sem=b_recv.at[t],
            device_id=(lax.rem(me + t, groups), rank),
            device_id_type=MESH,
        )

    for t in range(1, groups):
        back_copy(t).start()
    for t in range(1, groups):
        back_copy(t).wait()
    coming = (r_row == slots + in_slot) & (in_slot >= 0)
    result = jnp.where(coming, rows_back[from_group], jnp.where(going, 0.0, result))
    out_ref[...] = result.astype(BF16)


def per_device(
    suffix_cache,
    prompt_cache,
    query_first,
    fresh_first,
    query_second,
    fresh_second,
    out_weight,
    suffix_len,
    prompt_slot,
    moves,
):
    groups, ranks = lax.axis_size("grp"), lax.axis_size("tp")
    slots, features = query_first.shape
    prompts, plen = prompt_cache.shape[:2]
    cap = suffix_cache.shape[1]
    width = suffix_cache.shape[3]
    kv_heads = width // HD
    heads = features // HD
    cols = out_weight.shape[1] // ranks
    depth = out_weight.shape[0]
    vmem = pl.BlockSpec(memory_space=pltpu.VMEM)
    hbm = pl.BlockSpec(memory_space=pltpu.HBM)
    dma = pltpu.SemaphoreType.DMA
    out = pl.pallas_call(
        functools.partial(kernel, groups, ranks),
        out_shape=jax.ShapeDtypeStruct((2 * slots, cols), BF16),
        in_specs=[hbm] * 10,
        out_specs=vmem,
        scratch_shapes=[
            pltpu.VMEM((slots, kv_heads, cap, 2, HD), BF16),
            pltpu.VMEM((prompts, kv_heads, plen, 2, HD), BF16),
            pltpu.VMEM((ranks, depth, cols), BF16),
            pltpu.VMEM((slots, features), BF16),
            pltpu.VMEM((slots, 2, width), BF16),
            pltpu.VMEM((slots, features), BF16),
            pltpu.VMEM((slots, 2, width), BF16),
            pltpu.SMEM(suffix_len.shape, jnp.int32),
            pltpu.SMEM(prompt_slot.shape, jnp.int32),
            pltpu.SMEM(moves.shape, jnp.int32),
            pltpu.VMEM((2 * slots, features), F32),
            pltpu.VMEM((slots, 8, width), F32),
            pltpu.VMEM((8, width), F32),
            pltpu.VMEM((groups, heads + 8, HD), F32),
            pltpu.VMEM((ranks, 2 * slots, cols), BF16),
            pltpu.VMEM((ranks, 2 * slots, cols), BF16),
            pltpu.VMEM((groups, 1, cols), F32),
            dma((7,)),
            dma((prompts + slots, kv_heads)),
            dma((ranks,)),
            dma((groups,)),
            dma((groups,)),
            dma((ranks,)),
            dma((ranks,)),
            dma((groups,)),
            dma((groups,)),
        ],
        compiler_params=pltpu.CompilerParams(
            collective_id=0, has_side_effects=True, vmem_limit_bytes=67043328
        ),
    )(
        suffix_cache,
        prompt_cache,
        query_first,
        fresh_first,
        query_second,
        fresh_second,
        out_weight,
        suffix_len,
        prompt_slot,
        moves,
    )
    return out[:slots], out[slots:]


def solution(mesh):
    placed = (
        P("grp", None, None, "tp"),
        P("grp", None, None, "tp"),
        P("grp", "tp"),
        P("grp", None, "tp"),
        P("grp", "tp"),
        P("grp", None, "tp"),
        P("tp", None),
        P(),
        P("grp"),
        P(),
    )
    return jax.shard_map(
        per_device,
        mesh=mesh,
        in_specs=placed,
        out_specs=(P("grp", "tp"), P("grp", "tp")),
        check_vma=False,
    )
```

```python
import functools

import jax
import jax.numpy as jnp
from jax import lax
from jax.experimental import pallas as pl
from jax.experimental.pallas import tpu as pltpu
from jax.sharding import PartitionSpec as P

QH = 64
KVH = 8
HD = 128
MESH = pl.DeviceIdType.MESH
F32 = jnp.float32
BF16 = jnp.bfloat16


def kernel(
    groups,
    ranks,
    suffix_hbm,
    prompt_hbm,
    q1_hbm,
    f1_hbm,
    q2_hbm,
    f2_hbm,
    weight_hbm,
    lens_hbm,
    pslot_hbm,
    moves_hbm,
    out_ref,
    sbuf,
    pbuf,
    wbuf,
    q1_ref,
    f1_ref,
    q2_ref,
    f2_ref,
    lens_ref,
    pslot_ref,
    moves_ref,
    qs,
    fs,
    fresh_in,
    pack,
    packets,
    parts_out,
    parts_in,
    guest_out,
    guest_in,
    small_sem,
    kv_sem,
    w_sem,
    g_send,
    g_recv,
    r_send,
    r_recv,
    b_send,
    b_recv,
):
    me = lax.axis_index("grp")
    rank = lax.axis_index("tp")
    slots = q1_ref.shape[0]
    prompts = prompt_hbm.shape[0]
    features = q1_ref.shape[1]
    heads = features // HD
    share = QH // KVH
    kv_heads = heads // share
    width = kv_heads * HD
    cap = suffix_hbm.shape[1]
    plen = prompt_hbm.shape[1]
    cols = out_ref.shape[1]
    move_count = moves_ref.shape[0]

    cores = 2 if ranks % 2 == 0 else 1

    def rank_at(t):
        chip = lax.rem(rank // cores + t // cores, ranks // cores)
        return chip * cores + lax.rem(rank % cores + t % cores, cores)

    barrier = pltpu.get_barrier_semaphore()
    for u in range(groups):
        for t in range(ranks):
            if u or t:
                pl.semaphore_signal(
                    barrier,
                    inc=1,
                    device_id=(lax.rem(me + u, groups), rank_at(t)),
                    device_id_type=MESH,
                )

    small = [
        pltpu.make_async_copy(src, dst, small_sem.at[i])
        for i, (src, dst) in enumerate(
            [
                (moves_hbm, moves_ref),
                (q2_hbm, q2_ref),
                (f2_hbm, f2_ref),
                (lens_hbm, lens_ref),
                (pslot_hbm, pslot_ref),
                (q1_hbm, q1_ref),
                (f1_hbm, f1_ref),
            ]
        )
    ]
    kv_copies = []
    for k in range(kv_heads):
        lanes = pl.ds(k * HD, HD)
        for p in range(prompts):
            kv_copies.append(
                pltpu.make_async_copy(
                    prompt_hbm.at[p, :, :, lanes], pbuf.at[p, k], kv_sem.at[p, k]
                )
            )
        for s in range(slots):
            kv_copies.append(
                pltpu.make_async_copy(
                    suffix_hbm.at[s, :, :, lanes], sbuf.at[s, k], kv_sem.at[prompts + s, k]
                )
            )

    def weight_copy(t):
        j = rank_at(t)
        return pltpu.make_async_copy(
            weight_hbm.at[:, pl.ds(pl.multiple_of(j * cols, cols), cols)], wbuf.at[t], w_sem.at[t]
        )

    steps = list(range(cores, ranks)) + list(range(1, cores)) + [0]
    for copy in small:
        copy.start()
    for copy in kv_copies:
        copy.start()
    for t in steps:
        weight_copy(t).start()
    for copy in small:
        copy.wait()

    zero = jnp.int32(0)
    out_slot, into_group, in_slot, from_group = zero - 1, zero, zero - 1, zero
    for m in range(move_count):
        leaves = moves_ref[m, 0] == me
        enters = moves_ref[m, 2] == me
        out_slot = jnp.where(leaves, moves_ref[m, 1], out_slot)
        into_group = jnp.where(leaves, moves_ref[m, 2], into_group)
        in_slot = jnp.where(enters, moves_ref[m, 3], in_slot)
        from_group = jnp.where(enters, moves_ref[m, 0], from_group)

    rows = 2 * slots
    qs[0:slots] = q1_ref[...].astype(F32)
    qs[slots:rows] = q2_ref[...].astype(F32)
    stacked = jnp.concatenate([qs[:, j * HD : (j + 1) * HD] for j in range(heads)], 0).astype(BF16)
    total = heads * rows

    pick = (
        lax.broadcasted_iota(jnp.int32, (heads, total), 1)
        == lax.broadcasted_iota(jnp.int32, (heads, total), 0) * rows + slots + in_slot
    ).astype(F32).astype(BF16)
    pack[0:heads] = jnp.dot(pick, stacked, preferred_element_type=F32)
    pack[heads:] = jnp.zeros((8, HD), F32)
    fresh2 = [f2_ref[s].astype(F32) for s in range(slots)]
    own_fresh = jnp.zeros((2, width), F32)
    for s in range(slots):
        own_fresh = jnp.where(in_slot == s, fresh2[s], own_fresh)
    for k in range(kv_heads):
        pack[heads + 2 * k : heads + 2 * k + 2] = own_fresh[:, k * HD : (k + 1) * HD]
    packets[me] = pack[...].astype(BF16)

    pl.semaphore_wait(barrier, groups * ranks - 1)

    def gather_copy(t):
        return pltpu.make_async_remote_copy(
            src_ref=packets.at[me],
            dst_ref=packets.at[me],
            send_sem=g_send.at[t],
            recv_sem=g_recv.at[t],
            device_id=(lax.rem(me + t, groups), rank),
            device_id_type=MESH,
        )

    for t in range(1, groups):
        gather_copy(t).start()

    for s in range(slots):
        fs[s, 0:2] = f1_ref[s].astype(F32)
        fs[s, 2:4] = fresh2[s]
        fs[s, 4:8] = jnp.zeros((4, width), F32)

    mine = 2 * heads

    def source_of(r):
        s = r // mine
        k = (r % mine) // (2 * share)
        step = (r % (2 * share)) // share
        g = r % share
        return (k * share + g) * rows + step * slots + s

    swap = (
        source_of(lax.broadcasted_iota(jnp.int32, (total, total), 0))
        == lax.broadcasted_iota(jnp.int32, (total, total), 1)
    ).astype(F32).astype(BF16)
    back = (
        source_of(lax.broadcasted_iota(jnp.int32, (total, total), 1))
        == lax.broadcasted_iota(jnp.int32, (total, total), 0)
    ).astype(F32).astype(BF16)
    queries = jnp.dot(swap, stacked, preferred_element_type=F32)

    for copy in kv_copies:
        copy.wait()

    scale = HD ** (-0.5)
    low = -1e30
    nt = (((1,), (1,)), ((), ()))
    flat_p = pbuf.reshape(prompts, kv_heads, 2 * plen, HD)
    flat_s = sbuf.reshape(slots, kv_heads, 2 * cap, HD)
    p_col = lax.broadcasted_iota(jnp.int32, (1, 2 * plen), 1)
    s_col = lax.broadcasted_iota(jnp.int32, (1, 2 * cap), 1)
    f_col = lax.broadcasted_iota(jnp.int32, (1, 8), 1)
    p_valid = (p_col % 2) == 0
    s_even = (s_col % 2) == 0

    def attend(q, head_of, second, s, fval):
        wide = jnp.concatenate(
            [jnp.where(head_of == k, q, 0.0) for k in range(kv_heads)], 1
        ).astype(BF16)
        row = jnp.maximum(pslot_ref[s], 0)
        n = lens_ref[me * slots + s]
        xp = jnp.concatenate([flat_p[row, k] for k in range(kv_heads)], 1)
        xs = jnp.concatenate([flat_s[s, k] for k in range(kv_heads)], 1)
        xf = fval.astype(BF16)
        sp = lax.dot_general(wide, xp, nt, preferred_element_type=F32) * scale
        ss = lax.dot_general(wide, xs, nt, preferred_element_type=F32) * scale
        sf = lax.dot_general(wide, xf, nt, preferred_element_type=F32) * scale
        sp = jnp.where(p_valid, sp, low)
        ss = jnp.where(s_even & (s_col < 2 * n), ss, low)
        sf = jnp.where((f_col == 0) | ((f_col == 2) & second), sf, low)
        top = jnp.maximum(
            jnp.maximum(jnp.max(sp, 1, keepdims=True), jnp.max(ss, 1, keepdims=True)),
            jnp.max(sf, 1, keepdims=True),
        )
        ep, es, ef = jnp.exp(sp - top), jnp.exp(ss - top), jnp.exp(sf - top)
        inv = 1.0 / (
            jnp.sum(ep, 1, keepdims=True)
            + jnp.sum(es, 1, keepdims=True)
            + jnp.sum(ef, 1, keepdims=True)
        )

        def shifted(e):
            w = e * inv
            return jnp.concatenate(
                [pltpu.roll(w[:, i : i + HD], 1, 1) for i in range(0, e.shape[1], HD)], 1
            ).astype(BF16)

        mixed = jnp.dot(shifted(ep), xp, preferred_element_type=F32)
        mixed += jnp.dot(shifted(es), xs, preferred_element_type=F32)
        wf = (ef * inv).astype(BF16).astype(F32)
        mixed += wf[:, 0:1] * fval[1:2] + wf[:, 2:3] * fval[3:4]
        picked = mixed[:, :HD]
        for k in range(1, kv_heads):
            picked = jnp.where(head_of == k, mixed[:, k * HD : (k + 1) * HD], picked)
        return jnp.where(pslot_ref[s] >= 0, picked, 0.0)

    q_row = lax.broadcasted_iota(jnp.int32, (mine, 1), 0)
    results = [
        attend(
            queries[s * mine : (s + 1) * mine],
            q_row // (2 * share),
            (q_row % (2 * share)) >= share,
            s,
            fs[s],
        )
        for s in range(slots)
    ]
    attn = jnp.concatenate(results, 0).astype(BF16)
    attn = jnp.dot(back, attn, preferred_element_type=F32)

    for t in range(1, groups):
        gather_copy(t).wait()
    leaver = jnp.maximum(out_slot, 0)
    foreign = packets[into_group].astype(F32)
    fresh_in[...] = jnp.zeros((8, width), F32)
    for k in range(kv_heads):
        fresh_in[2:4, k * HD : (k + 1) * HD] = foreign[heads + 2 * k : heads + 2 * k + 2]
    fresh_in[0:2] = f1_ref[leaver].astype(F32)
    h_row = lax.broadcasted_iota(jnp.int32, (heads, 1), 0)
    guest = attend(foreign[:heads], h_row // share, h_row >= 0, leaver, fresh_in[...])
    r_row = lax.broadcasted_iota(jnp.int32, (rows, 1), 0)
    going = (r_row == slots + out_slot) & (out_slot >= 0)
    attn = jnp.concatenate(
        [
            jnp.where(going, guest[j : j + 1], attn[j * rows : (j + 1) * rows])
            for j in range(heads)
        ],
        1,
    ).astype(BF16)

    def part_copy(t):
        return pltpu.make_async_remote_copy(
            src_ref=parts_out.at[t],
            dst_ref=parts_in.at[t],
            send_sem=r_send.at[t],
            recv_sem=r_recv.at[t],
            device_id=(me, rank_at(t)),
            device_id_type=MESH,
        )

    def guest_copy(u, t):
        return pltpu.make_async_remote_copy(
            src_ref=guest_out.at[t],
            dst_ref=guest_in.at[me, t],
            send_sem=b_send.at[u, t],
            recv_sem=b_recv.at[u, t],
            device_id=(lax.rem(me + u, groups), rank_at(t)),
            device_id_type=MESH,
        )

    guest_in[me] = jnp.zeros(guest_in.shape[1:], BF16)
    result = None
    for t in steps:
        weight_copy(t).wait()
        part = jnp.dot(attn, wbuf[t], preferred_element_type=F32)
        alone = jnp.sum(jnp.where(going, part, 0.0), 0, keepdims=True)
        guest_out[t] = jnp.concatenate(
            [alone[:, i : i + HD] for i in range(0, cols, HD)], 0
        ).astype(BF16)
        if t:
            parts_out[t] = part.astype(BF16)
            part_copy(t).start()
        else:
            result = part
        for u in range(1, groups):
            guest_copy(u, t).start()
    for t in range(1, ranks):
        part_copy(t).wait()
        result += parts_in[t].astype(F32)
    for t in steps:
        for u in range(1, groups):
            guest_copy(u, t).wait()
    arrived = jnp.sum(guest_in[from_group].astype(F32), 0)
    arrived = jnp.concatenate([arrived[i : i + 1] for i in range(cols // HD)], 1)
    coming = (r_row == slots + in_slot) & (in_slot >= 0)
    result = jnp.where(coming, arrived, jnp.where(going, 0.0, result))
    out_ref[...] = result.astype(BF16)


def per_device(
    suffix_cache,
    prompt_cache,
    query_first,
    fresh_first,
    query_second,
    fresh_second,
    out_weight,
    suffix_len,
    prompt_slot,
    moves,
):
    groups, ranks = lax.axis_size("grp"), lax.axis_size("tp")
    slots, features = query_first.shape
    prompts, plen = prompt_cache.shape[:2]
    cap = suffix_cache.shape[1]
    width = suffix_cache.shape[3]
    kv_heads = width // HD
    heads = features // HD
    cols = out_weight.shape[1] // ranks
    depth = out_weight.shape[0]
    vmem = pl.BlockSpec(memory_space=pltpu.VMEM)
    hbm = pl.BlockSpec(memory_space=pltpu.HBM)
    dma = pltpu.SemaphoreType.DMA
    out = pl.pallas_call(
        functools.partial(kernel, groups, ranks),
        out_shape=pltpu.VMEM((2 * slots, cols), BF16),
        in_specs=[hbm] * 10,
        out_specs=vmem,
        scratch_shapes=[
            pltpu.VMEM((slots, kv_heads, cap, 2, HD), BF16),
            pltpu.VMEM((prompts, kv_heads, plen, 2, HD), BF16),
            pltpu.VMEM((ranks, depth, cols), BF16),
            pltpu.VMEM((slots, features), BF16),
            pltpu.VMEM((slots, 2, width), BF16),
            pltpu.VMEM((slots, features), BF16),
            pltpu.VMEM((slots, 2, width), BF16),
            pltpu.SMEM(suffix_len.shape, jnp.int32),
            pltpu.SMEM(prompt_slot.shape, jnp.int32),
            pltpu.SMEM(moves.shape, jnp.int32),
            pltpu.VMEM((2 * slots, features), F32),
            pltpu.VMEM((slots, 8, width), F32),
            pltpu.VMEM((8, width), F32),
            pltpu.VMEM((heads + 8, HD), F32),
            pltpu.VMEM((groups, heads + 8, HD), BF16),
            pltpu.VMEM((ranks, 2 * slots, cols), BF16),
            pltpu.VMEM((ranks, 2 * slots, cols), BF16),
            pltpu.VMEM((ranks, cols // HD, HD), BF16),
            pltpu.VMEM((groups, ranks, cols // HD, HD), BF16),
            dma((7,)),
            dma((prompts + slots, kv_heads)),
            dma((ranks,)),
            dma((groups,)),
            dma((groups,)),
            dma((ranks,)),
            dma((ranks,)),
            dma((groups, ranks)),
            dma((groups, ranks)),
        ],
        compiler_params=pltpu.CompilerParams(
            collective_id=0, has_side_effects=True, vmem_limit_bytes=48 * 1024 * 1024
        ),
    )(
        *[
            pltpu.with_memory_space_constraint(x, pltpu.HBM)
            for x in (
                suffix_cache,
                prompt_cache,
                query_first,
                fresh_first,
                query_second,
                fresh_second,
                out_weight,
                suffix_len,
                prompt_slot,
                moves,
            )
        ]
    )
    return out[:slots], out[slots:]


def solution(mesh):
    placed = (
        P("grp", None, None, "tp"),
        P("grp", None, None, "tp"),
        P("grp", "tp"),
        P("grp", None, "tp"),
        P("grp", "tp"),
        P("grp", None, "tp"),
        P("tp", None),
        P(),
        P("grp"),
        P(),
    )
    return jax.shard_map(
        per_device,
        mesh=mesh,
        in_specs=placed,
        out_specs=(P("grp", "tp"), P("grp", "tp")),
        check_vma=False,
    )
```
